256 devices in a mesh: bfly: 256 (over z, x, y, core).
Axes of the slice: x: 4, y: 4, z: 8, core: 2. Of those that a mesh axis runs over, the one named last changes fastest.
Arguments:
- coeffs: float32 [256, 384, 1024], P('bfly'), may hold values from -6 to 6
- transfers: float32 [256, 8, 2, 384, 384], P('bfly'), may hold values from -0.21875 to 0.21875
Outputs:
- result: float32 [256, 384, 1024], P('bfly')
The draws below stay inside these ranges and needn't reach their ends.
All inputs are finite; a program needn't handle non-finite values.
Results may differ from the reference program's by a relative error of at most 0.00014.
Values sent between devices are 32-bit elements; how exact they have to be, the bound alone decides.
No kernel may reach another device: no remote copies, remote signals or barrier semaphores. Data moves between devices by JAX's collectives and lax.ppermute only.
A program may use at most 64 MiB of HBM per device.

```python
import jax
import jax.numpy as jnp
from jax import lax

RANK = 384
COLS = 1024
LEVELS = 8
NODES = 256
N_BFLY = 256


def level_of(key, extent, shards, low, high):
    gain = 1.0
    for position, blocks in shards:
        draws = jax.random.uniform(jax.random.fold_in(jax.random.fold_in(key, 6), position), (blocks,), jnp.float32, low / len(shards), high / len(shards))
        gain = gain * jnp.repeat(jnp.exp(draws), extent[position] // blocks).reshape((-1,) + (1,) * (len(extent) - 1 - position))
    return gain


def scatter_about(key, shape, width, most, cuts=(), kind=jnp.bfloat16):
    values = jax.random.normal(key, shape, jnp.float32) * width
    if len(cuts) > 0:
        values = level_of(key, shape, cuts, -0.22, 0.18) * values
    return jnp.clip(values, min=-most, max=most).astype(kind)


def setup_inputs(seed: int = 0) -> dict:
    key_list = jax.random.split(jax.random.key(seed), 3)
    coeffs = scatter_about(key_list[0], (NODES, RANK, COLS), 1.0, 6.0, ((0, 256),), jnp.float32)
    transfers = scatter_about(key_list[1], (NODES, LEVELS, 2, RANK, RANK), (2 * RANK) ** -0.5, 0.21875, ((0, 256),), jnp.float32)
    return {"coeffs": coeffs, "transfers": transfers}


def reference(coeffs, transfers):
    bit_count = N_BFLY.bit_length() - 1
    node_ids = jnp.arange(N_BFLY, dtype=jnp.int32)
    state = coeffs
    for depth_level in range(LEVELS):
        bit_value = 1 << (depth_level % bit_count)
        partner = jnp.bitwise_xor(node_ids, bit_value).astype(jnp.int32)
        own_term = jnp.einsum("nij,njc->nic", transfers[:, depth_level, 0], state, precision=lax.Precision.HIGHEST)
        sent_term = jnp.einsum("nij,njc->nic", transfers[:, depth_level, 1], state, precision=lax.Precision.HIGHEST)
        state = own_term + sent_term[partner]
    return state
```

```python
import jax
import jax.numpy as jnp
from jax import lax
from jax.sharding import PartitionSpec as P

LEVELS = 8
WIDTHS = (128, 128, 256, 256, 256)
ORDER = (
    (0, 0), (1, 0), (2, 0), (0, 1), (3, 0), (4, 0), (1, 1), (0, 2), (1, 2), (0, 3), (2, 1), (1, 3),
    (0, 4), (3, 1), (1, 4), (0, 5), (2, 2), (1, 5), (0, 6), (3, 2), (2, 3), (1, 6), (0, 7), (3, 3),
    (4, 1), (2, 4), (1, 7), (0, 8), (4, 2), (3, 4), (2, 5), (1, 8), (4, 3), (3, 5), (2, 6), (4, 4),
    (4, 5), (3, 6), (2, 7), (4, 6), (3, 7), (2, 8), (4, 7), (3, 8), (4, 8),
)


def partner(block, axis, stride):
    count = lax.axis_size(axis)
    route = []
    for low in range(count):
        high = low | 1 << stride
        if high != low and high < count:
            route += [(low, high), (high, low)]
    return lax.ppermute(block, axis, route)


def apply_matrix(matrix, values):
    return jnp.dot(matrix, values, preferred_element_type=jnp.float32, precision=lax.Precision.HIGH)


def on_device(coeffs, transfers):
    bit_count = lax.axis_size("bfly").bit_length() - 1
    starts = [sum(WIDTHS[:i]) for i in range(len(WIDTHS))]
    parts = [(coeffs[0][:, s:s + w],) for s, w in zip(starts, WIDTHS)]
    last = None
    for chunk, level in ORDER:
        ready = parts[chunk]
        if last is not None:
            ready = lax.optimization_barrier(ready + (last,))[:-1]
        current = ready[0] if len(ready) == 1 else ready[0] + ready[1]
        if level == LEVELS:
            parts[chunk] = last = current
            continue
        outgoing = last = apply_matrix(transfers[0, level, 1], current)
        arrived = partner(outgoing, "bfly", level % bit_count)
        parts[chunk] = (apply_matrix(transfers[0, level, 0], current), arrived)
    return jnp.concatenate(parts, axis=1)[None]


def solution(mesh):
    return jax.shard_map(
        on_device,
        mesh=mesh,
        in_specs=(P("bfly", None, None), P("bfly", None, None, None, None)),
        out_specs=P("bfly", None, None),
        check_vma=False,
    )
```

```python
import functools
import jax
import jax.numpy as jnp
from jax import lax
from jax.experimental import pallas as pl
from jax.experimental.pallas import tpu as pltpu
from jax.sharding import PartitionSpec as P

LEVELS = 8
WIDTHS = (128, 128, 256, 256, 256)
ORDER = (
    (0, 0), (1, 0), (2, 0), (0, 1), (3, 0), (4, 0), (1, 1), (0, 2), (1, 2), (0, 3), (2, 1), (1, 3),
    (0, 4), (3, 1), (1, 4), (0, 5), (2, 2), (1, 5), (0, 6), (3, 2), (2, 3), (1, 6), (0, 7), (3, 3),
    (4, 1), (2, 4), (1, 7), (0, 8), (4, 2), (3, 4), (2, 5), (1, 8), (4, 3), (3, 5), (2, 6), (4, 4),
    (4, 5), (3, 6), (2, 7), (4, 6), (3, 7), (2, 8), (4, 7), (3, 8), (4, 8),
)
ANY = pl.BlockSpec(memory_space=pl.ANY)
VMEM = pl.BlockSpec(memory_space=pltpu.VMEM)
PARAMS = pltpu.CompilerParams(vmem_limit_bytes=12 << 20)
TOKEN = pltpu.VMEM((8, 128), jnp.float32)
CHEAP = pl.CostEstimate(flops=1, bytes_accessed=1, transcendentals=0)


def partner(block, axis, stride):
    count = lax.axis_size(axis)
    route = []
    for low in range(count):
        high = low | 1 << stride
        if high != low and high < count:
            route += [(low, high), (high, low)]
    return lax.ppermute(block, axis, route)


def on_chip(values):
    return pltpu.with_memory_space_constraint(values, pltpu.VMEM)


def split(values):
    high = values.astype(jnp.bfloat16)
    return high, (values - high.astype(jnp.float32)).astype(jnp.bfloat16)


def in_hbm(values):
    return pltpu.with_memory_space_constraint(values, pltpu.HBM)


def split_kernel(token_ref, t_ref, out_ref, next_ref):
    rank = t_ref.shape[-1]
    rows = 128
    for which in range(2):
        @pl.loop(0, rank // rows)
        def _(i):
            here = pl.ds(pl.multiple_of(i * rows, rows), rows)
            there = pl.ds(pl.multiple_of(which * rank + i * rows, rows), rows)
            high, low = split(t_ref[0, 0, which, here])
            out_ref[there, :rank] = high
            out_ref[there, rank:2 * rank] = high
            out_ref[there, 2 * rank:] = low
    next_ref[...] = jnp.zeros_like(next_ref)


def split_matrices(token, transfers, level):
    rank = transfers.shape[-1]
    return pl.pallas_call(
        split_kernel,
        grid=(1,),
        out_shape=(pltpu.VMEM((2 * rank, 3 * rank), jnp.bfloat16), TOKEN),
        in_specs=[VMEM, pl.BlockSpec((1, 1, 2, rank, rank), lambda i: (0, level, 0, 0, 0))],
        out_specs=(VMEM, VMEM),
        cost_estimate=CHEAP,
        compiler_params=PARAMS,
        name="split_matrices",
    )(on_chip(token), in_hbm(transfers))


def multiply(t_ref, current, send_ref, keep_ref, stacked):
    rank = current.shape[0]
    high, low = split(current)
    stacked[:rank] = high
    stacked[rank:2 * rank] = low
    stacked[2 * rank:] = high

    @pl.loop(0, 2)
    def _(which):
        rows = pl.ds(pl.multiple_of(which * rank, rank), rank)
        product = jnp.dot(t_ref[rows], stacked[...], preferred_element_type=jnp.float32)

        @pl.when(which == 0)
        def _():
            keep_ref[...] = product

        @pl.when(which == 1)
        def _():
            send_ref[...] = product


def first_kernel(start, token_ref, t_ref, c_ref, send_ref, keep_ref, next_ref, stacked, block, sem):
    copy = pltpu.make_async_copy(c_ref.at[0, :, pl.ds(start, block.shape[1])], block, sem)
    copy.start()
    copy.wait()
    multiply(t_ref, block[...], send_ref, keep_ref, stacked)
    next_ref[...] = jnp.zeros_like(next_ref)


def level_kernel(token_ref, t_ref, kept_ref, arrived_ref, send_ref, keep_ref, next_ref, stacked):
    multiply(t_ref, kept_ref[...] + arrived_ref[...], send_ref, keep_ref, stacked)
    next_ref[...] = jnp.zeros_like(next_ref)


def stage(name, kernel, operands, specs, width, scratch=()):
    rank = operands[1].shape[0] // 2
    block = pltpu.VMEM((rank, width), jnp.float32)
    return pl.pallas_call(
        kernel,
        out_shape=(block, block, TOKEN),
        in_specs=specs,
        out_specs=(VMEM, VMEM, VMEM),
        scratch_shapes=[pltpu.VMEM((3 * rank, width), jnp.bfloat16), *scratch],
        cost_estimate=CHEAP,
        compiler_params=PARAMS,
        name=name,
    )(*operands)


def first_level(token, matrices, coeffs, start, width):
    scratch = (pltpu.VMEM((coeffs.shape[1], width), jnp.float32), pltpu.SemaphoreType.DMA)
    operands = (on_chip(token), on_chip(matrices), in_hbm(coeffs))
    kernel = functools.partial(first_kernel, start)
    return stage("first_level", kernel, operands, [VMEM, VMEM, ANY], width, scratch)


def next_level(token, matrices, kept, arrived):
    operands = tuple(map(on_chip, (token, matrices, kept, arrived)))
    return stage("next_level", level_kernel, operands, [VMEM] * 4, kept.shape[1])


def write_kernel(start, token_ref, kept_ref, arrived_ref, *refs):
    out_ref, next_ref, block, sem = refs[-4:]
    block[...] = kept_ref[...] + arrived_ref[...]
    copy = pltpu.make_async_copy(block, out_ref.at[0, :, pl.ds(start, block.shape[1])], sem)
    copy.start()
    copy.wait()
    next_ref[...] = jnp.zeros_like(next_ref)


def write_result(token, kept, arrived, start, shape, result):
    parts = tuple(map(on_chip, (token, kept, arrived))) + (() if result is None else (result,))
    return pl.pallas_call(
        functools.partial(write_kernel, start),
        out_shape=(jax.ShapeDtypeStruct(shape, jnp.float32), TOKEN),
        in_specs=[VMEM] * 3 + [ANY] * (len(parts) - 3),
        out_specs=(ANY, VMEM),
        scratch_shapes=[pltpu.VMEM(kept.shape, jnp.float32), pltpu.SemaphoreType.DMA],
        input_output_aliases={} if result is None else {3: 0},
        cost_estimate=CHEAP,
        compiler_params=PARAMS,
        name="write_result",
    )(*parts)


def on_device(coeffs, transfers):
    bit_count = lax.axis_size("bfly").bit_length() - 1
    starts = [sum(WIDTHS[:i]) for i in range(len(WIDTHS))]
    parts = [()] * len(WIDTHS)
    token = jnp.zeros(TOKEN.shape, TOKEN.dtype)
    first, token = split_matrices(token, transfers, 0)
    matrices = [first]
    result = None
    for chunk, level in ORDER:
        if level == LEVELS:
            result, token = write_result(token, *parts[chunk], starts[chunk], coeffs.shape, result)
            continue
        if level == 0:
            stepped = first_level(token, matrices[0], coeffs, starts[chunk], WIDTHS[chunk])
        else:
            stepped = next_level(token, matrices[level], *parts[chunk])
        outgoing, kept, token = stepped
        parts[chunk] = (kept, partner(outgoing, "bfly", level % bit_count))
        if len(matrices) == level + 1 < LEVELS:
            following, token = split_matrices(token, transfers, level + 1)
            matrices.append(following)
    return result


def solution(mesh):
    return jax.shard_map(
        on_device,
        mesh=mesh,
        in_specs=(P("bfly", None, None), P("bfly", None, None, None, None)),
        out_specs=P("bfly", None, None),
        check_vma=False,
    )
```

```python
import functools
import jax
import jax.numpy as jnp
from jax import lax
from jax.experimental import pallas as pl
from jax.experimental.pallas import tpu as pltpu
from jax.sharding import PartitionSpec as P

LEVELS = 8
WIDTHS = (128, 256, 128, 256, 256)
ORDER = (
    (0, 0), (0, 1), (2, 0), (0, 2), (2, 1), (4, 0), (0, 3), (2, 2), (4, 1), (0, 4), (3, 0), (2, 3),
    (0, 5), (4, 2), (2, 4), (0, 6), (3, 1), (4, 3), (2, 5), (0, 7), (4, 4), (3, 2), (2, 6), (4, 5),
    (3, 3), (1, 0), (2, 7), (1, 1), (3, 4), (4, 6), (2, 8), (1, 2), (3, 5), (1, 3), (4, 7), (0, 8),
    (1, 4), (1, 5), (3, 6), (1, 6), (4, 8), (3, 7), (1, 7), (3, 8), (1, 8),
)
ANY = pl.BlockSpec(memory_space=pl.ANY)
VMEM = pl.BlockSpec(memory_space=pltpu.VMEM)
PARAMS = pltpu.CompilerParams(vmem_limit_bytes=12 << 20)
TOKEN = pltpu.VMEM((8, 128), jnp.float32)
CHEAP = pl.CostEstimate(flops=1 << 33, bytes_accessed=1 << 10, transcendentals=0)


def partner(block, axis, stride):
    count = lax.axis_size(axis)
    route = []
    for low in range(count):
        high = low | 1 << stride
        if high != low and high < count:
            route += [(low, high), (high, low)]
    return lax.ppermute(block, axis, route)


def on_chip(values):
    return pltpu.with_memory_space_constraint(values, pltpu.VMEM)


def split(values):
    high = values.astype(jnp.bfloat16)
    return high, (values - high.astype(jnp.float32)).astype(jnp.bfloat16)


def in_hbm(values):
    return pltpu.with_memory_space_constraint(values, pltpu.HBM)


def split_kernel(token_ref, t_ref, out_ref, next_ref):
    rank = t_ref.shape[-1]
    rows = 16
    for which in range(2):
        @pl.loop(0, rank // rows)
        def _(i):
            here = pl.ds(pl.multiple_of(i * rows, rows), rows)
            there = pl.ds(pl.multiple_of(which * rank + i * rows, rows), rows)
            high, low = split(t_ref[0, 0, which, here])
            out_ref[there, :rank] = high
            out_ref[there, rank:2 * rank] = high
            out_ref[there, 2 * rank:] = low
    next_ref[...] = jnp.zeros_like(next_ref)


def split_matrices(token, transfers, level):
    rank = transfers.shape[-1]
    return pl.pallas_call(
        split_kernel,
        grid=(1,),
        out_shape=(pltpu.VMEM((2 * rank, 3 * rank), jnp.bfloat16), TOKEN),
        in_specs=[VMEM, pl.BlockSpec((1, 1, 2, rank, rank), lambda i: (0, level, 0, 0, 0))],
        out_specs=(VMEM, VMEM),
        cost_estimate=CHEAP,
        compiler_params=PARAMS,
        name="split_matrices",
    )(on_chip(token), in_hbm(transfers))


def multiply(t_ref, part_refs, send_ref, keep_ref, stacked):
    rank = send_ref.shape[0]
    step = 64

    @pl.loop(0, rank // step)
    def _(i):
        here = pl.multiple_of(i * step, step)
        current = part_refs[0][pl.ds(here, step)]
        for part_ref in part_refs[1:]:
            current = current + part_ref[pl.ds(here, step)]
        high, low = split(current)
        stacked[pl.ds(here, step)] = high
        stacked[pl.ds(pl.multiple_of(here + rank, step), step)] = low
        stacked[pl.ds(pl.multiple_of(here + 2 * rank, step), step)] = high

    rows = rank // 2

    @pl.loop(0, 4)
    def _(i):
        source = pl.ds(pl.multiple_of(i * rows, rows), rows)
        product = jnp.dot(t_ref[source], stacked[...], preferred_element_type=jnp.float32)

        @pl.when(i < 2)
        def _():
            keep_ref[source] = product

        @pl.when(i >= 2)
        def _():
            send_ref[pl.ds(pl.multiple_of((i - 2) * rows, rows), rows)] = product


def first_kernel(start, token_ref, t_ref, c_ref, send_ref, keep_ref, next_ref, stacked, block, sem):
    copy = pltpu.make_async_copy(c_ref.at[0, :, pl.ds(start, block.shape[1])], block, sem)
    copy.start()
    copy.wait()
    multiply(t_ref, (block,), send_ref, keep_ref, stacked)
    next_ref[...] = jnp.zeros_like(next_ref)


def level_kernel(token_ref, t_ref, kept_ref, arrived_ref, send_ref, keep_ref, next_ref, stacked):
    multiply(t_ref, (kept_ref, arrived_ref), send_ref, keep_ref, stacked)
    next_ref[...] = jnp.zeros_like(next_ref)


def stage(name, kernel, operands, specs, width, scratch=()):
    rank = operands[1].shape[0] // 2
    block = pltpu.VMEM((rank, width), jnp.float32)
    return pl.pallas_call(
        kernel,
        out_shape=(block, block, TOKEN),
        in_specs=specs,
        out_specs=(VMEM, VMEM, VMEM),
        scratch_shapes=[pltpu.VMEM((3 * rank, width), jnp.bfloat16), *scratch],
        cost_estimate=CHEAP,
        compiler_params=PARAMS,
        name=name,
    )(*operands)


def first_level(token, matrices, coeffs, start, width):
    scratch = (pltpu.VMEM((coeffs.shape[1], width), jnp.float32), pltpu.SemaphoreType.DMA)
    operands = (on_chip(token), on_chip(matrices), in_hbm(coeffs))
    kernel = functools.partial(first_kernel, start)
    return stage("first_level", kernel, operands, [VMEM, VMEM, ANY], width, scratch)


def next_level(token, matrices, kept, arrived):
    operands = tuple(map(on_chip, (token, matrices, kept, arrived)))
    return stage("next_level", level_kernel, operands, [VMEM] * 4, kept.shape[1])


def write_kernel(start, token_ref, kept_ref, arrived_ref, *refs):
    out_ref, next_ref, block, sem = refs[-4:]
    step = 64

    @pl.loop(0, block.shape[0] // step)
    def _(i):
        here = pl.ds(pl.multiple_of(i * step, step), step)
        block[here] = kept_ref[here] + arrived_ref[here]

    copy = pltpu.make_async_copy(block, out_ref.at[0, :, pl.ds(start, block.shape[1])], sem)
    copy.start()
    copy.wait()
    next_ref[...] = jnp.zeros_like(next_ref)


def write_result(token, kept, arrived, start, shape, result):
    parts = tuple(map(on_chip, (token, kept, arrived))) + (() if result is None else (result,))
    return pl.pallas_call(
        functools.partial(write_kernel, start),
        out_shape=(jax.ShapeDtypeStruct(shape, jnp.float32), TOKEN),
        in_specs=[VMEM] * 3 + [ANY] * (len(parts) - 3),
        out_specs=(ANY, VMEM),
        scratch_shapes=[pltpu.VMEM(kept.shape, jnp.float32), pltpu.SemaphoreType.DMA],
        input_output_aliases={} if result is None else {3: 0},
        cost_estimate=CHEAP,
        compiler_params=PARAMS,
        name="write_result",
    )(*parts)


def on_device(coeffs, transfers):
    bit_count = lax.axis_size("bfly").bit_length() - 1
    starts = [sum(WIDTHS[:i]) for i in range(len(WIDTHS))]
    parts = [()] * len(WIDTHS)
    token = jnp.zeros(TOKEN.shape, TOKEN.dtype)
    first, token = split_matrices(token, transfers, 0)
    matrices = [first]
    result = None
    for chunk, level in ORDER:
        if level == LEVELS:
            result, token = write_result(token, *parts[chunk], starts[chunk], coeffs.shape, result)
            continue
        if level == 0:
            stepped = first_level(token, matrices[0], coeffs, starts[chunk], WIDTHS[chunk])
        else:
            stepped = next_level(token, matrices[level], *parts[chunk])
        outgoing, kept, token = stepped
        parts[chunk] = (kept, partner(outgoing, "bfly", level % bit_count))
        if len(matrices) == level + 1 < LEVELS:
            following, token = split_matrices(token, transfers, level + 1)
            matrices.append(following)
    return result


def solution(mesh):
    return jax.shard_map(
        on_device,
        mesh=mesh,
        in_specs=(P("bfly", None, None), P("bfly", None, None, None, None)),
        out_specs=P("bfly", None, None),
        check_vma=False,
    )
```

```python
import functools
import jax
import jax.numpy as jnp
from jax import lax
from jax.experimental import pallas as pl
from jax.experimental.pallas import tpu as pltpu
from jax.sharding import PartitionSpec as P

LEVELS = 8
WIDTHS = (128, 128, 256, 256, 256)
ORDER = (
    (3, 0), (3, 1), (0, 0), (3, 2), (1, 0), (2, 0), (0, 1), (3, 3), (0, 2), (1, 1), (3, 4), (4, 0),
    (1, 2), (0, 3), (3, 5), (0, 4), (1, 3), (4, 1), (3, 6), (0, 5), (1, 4), (4, 2), (1, 5), (0, 6),
    (4, 3), (3, 7), (2, 1), (4, 4), (2, 2), (4, 5), (1, 6), (2, 3), (1, 7), (2, 4), (0, 7), (1, 8),
    (2, 5), (4, 6), (2, 6), (3, 8), (4, 7), (2, 7), (0, 8), (4, 8), (2, 8),
)
ANY = pl.BlockSpec(memory_space=pl.ANY)
VMEM = pl.BlockSpec(memory_space=pltpu.VMEM)
PARAMS = pltpu.CompilerParams(vmem_limit_bytes=12 << 20)
TOKEN = pltpu.VMEM((8, 128), jnp.float32)
COST = pl.CostEstimate(flops=1 << 33, bytes_accessed=1 << 10, transcendentals=0)


def partner(block, axis, stride):
    count = lax.axis_size(axis)
    route = []
    for low in range(count):
        high = low | 1 << stride
        if high != low and high < count:
            route += [(low, high), (high, low)]
    return lax.ppermute(block, axis, route)


def on_chip(values):
    return pltpu.with_memory_space_constraint(values, pltpu.VMEM)


def split(values):
    high = values.astype(jnp.bfloat16)
    return high, (values - high.astype(jnp.float32)).astype(jnp.bfloat16)


def in_hbm(values):
    return pltpu.with_memory_space_constraint(values, pltpu.HBM)


def split_kernel(token_ref, t_ref, out_ref, next_ref):
    rank = t_ref.shape[-1]
    rows = 16
    for which in range(2):
        @pl.loop(0, rank // rows)
        def _(i):
            here = pl.ds(pl.multiple_of(i * rows, rows), rows)
            there = pl.ds(pl.multiple_of(which * rank + i * rows, rows), rows)
            high, low = split(t_ref[0, 0, which, here])
            out_ref[there, :rank] = high
            out_ref[there, rank:2 * rank] = high
            out_ref[there, 2 * rank:] = low
    next_ref[...] = jnp.zeros_like(next_ref)


def split_matrices(token, transfers, level):
    rank = transfers.shape[-1]
    return pl.pallas_call(
        split_kernel,
        grid=(1,),
        out_shape=(pltpu.VMEM((2 * rank, 3 * rank), jnp.bfloat16), TOKEN),
        in_specs=[VMEM, pl.BlockSpec((1, 1, 2, rank, rank), lambda i: (0, level, 0, 0, 0))],
        out_specs=(VMEM, VMEM),
        cost_estimate=COST,
        compiler_params=PARAMS,
        name="split_matrices",
    )(on_chip(token), in_hbm(transfers))


def multiply(blocks, t_ref, part_refs, send_ref, keep_ref, stacked):
    rank = send_ref.shape[0]
    step = 48

    @pl.loop(0, rank // step)
    def _(i):
        here = pl.multiple_of(i * step, step)
        current = part_refs[0][pl.ds(here, step)]
        for part_ref in part_refs[1:]:
            current = current + part_ref[pl.ds(here, step)]
        high, low = split(current)
        stacked[pl.ds(here, step)] = high
        stacked[pl.ds(pl.multiple_of(here + rank, step), step)] = low
        stacked[pl.ds(pl.multiple_of(here + 2 * rank, step), step)] = high

    rows = rank // blocks

    @pl.loop(0, 2 * blocks)
    def _(i):
        source = pl.ds(pl.multiple_of(i * rows, rows), rows)
        product = jnp.dot(t_ref[source], stacked[...], preferred_element_type=jnp.float32)

        @pl.when(i < blocks)
        def _():
            keep_ref[source] = product

        @pl.when(i >= blocks)
        def _():
            send_ref[pl.ds(pl.multiple_of((i - blocks) * rows, rows), rows)] = product


def first_kernel(start, token_ref, t_ref, c_ref, send_ref, keep_ref, next_ref, stacked, block, sem):
    copy = pltpu.make_async_copy(c_ref.at[0, :, pl.ds(start, block.shape[1])], block, sem)
    copy.start()
    copy.wait()
    multiply(2, t_ref, (block,), send_ref, keep_ref, stacked)
    next_ref[...] = jnp.zeros_like(next_ref)


def level_kernel(token_ref, t_ref, kept_ref, arrived_ref, send_ref, keep_ref, next_ref, stacked):
    multiply(1, t_ref, (kept_ref, arrived_ref), send_ref, keep_ref, stacked)
    next_ref[...] = jnp.zeros_like(next_ref)


def stage(name, kernel, operands, specs, width, scratch=()):
    rank = operands[1].shape[0] // 2
    block = pltpu.VMEM((rank, width), jnp.float32)
    return pl.pallas_call(
        kernel,
        out_shape=(block, block, TOKEN),
        in_specs=specs,
        out_specs=(VMEM, VMEM, VMEM),
        scratch_shapes=[pltpu.VMEM((3 * rank, width), jnp.bfloat16), *scratch],
        cost_estimate=COST,
        compiler_params=PARAMS,
        name=name,
    )(*operands)


def first_level(token, matrices, coeffs, start, width):
    scratch = (pltpu.VMEM((coeffs.shape[1], width), jnp.float32), pltpu.SemaphoreType.DMA)
    operands = (on_chip(token), on_chip(matrices), in_hbm(coeffs))
    kernel = functools.partial(first_kernel, start)
    return stage("first_level", kernel, operands, [VMEM, VMEM, ANY], width, scratch)


def next_level(token, matrices, kept, arrived):
    operands = tuple(map(on_chip, (token, matrices, kept, arrived)))
    return stage("next_level", level_kernel, operands, [VMEM] * 4, kept.shape[1])


def write_kernel(start, token_ref, kept_ref, arrived_ref, *refs):
    out_ref, next_ref, block, sem = refs[-4:]
    step = 48

    @pl.loop(0, block.shape[0] // step)
    def _(i):
        here = pl.ds(pl.multiple_of(i * step, step), step)
        block[here] = kept_ref[here] + arrived_ref[here]

    copy = pltpu.make_async_copy(block, out_ref.at[0, :, pl.ds(start, block.shape[1])], sem)
    copy.start()
    copy.wait()
    next_ref[...] = jnp.zeros_like(next_ref)


def write_result(token, kept, arrived, start, shape, result):
    parts = tuple(map(on_chip, (token, kept, arrived))) + (() if result is None else (result,))
    return pl.pallas_call(
        functools.partial(write_kernel, start),
        out_shape=(jax.ShapeDtypeStruct(shape, jnp.float32), TOKEN),
        in_specs=[VMEM] * 3 + [ANY] * (len(parts) - 3),
        out_specs=(ANY, VMEM),
        scratch_shapes=[pltpu.VMEM(kept.shape, jnp.float32), pltpu.SemaphoreType.DMA],
        input_output_aliases={} if result is None else {3: 0},
        cost_estimate=COST,
        compiler_params=PARAMS,
        name="write_result",
    )(*parts)


def on_device(coeffs, transfers):
    bit_count = lax.axis_size("bfly").bit_length() - 1
    starts = [sum(WIDTHS[:i]) for i in range(len(WIDTHS))]
    parts = [()] * len(WIDTHS)
    token = jnp.zeros(TOKEN.shape, TOKEN.dtype)
    first, token = split_matrices(token, transfers, 0)
    matrices = [first]
    result = None
    for chunk, level in ORDER:
        if level == LEVELS:
            result, token = write_result(token, *parts[chunk], starts[chunk], coeffs.shape, result)
            continue
        if level == 0:
            stepped = first_level(token, matrices[0], coeffs, starts[chunk], WIDTHS[chunk])
        else:
            stepped = next_level(token, matrices[level], *parts[chunk])
        outgoing, kept, token = stepped
        parts[chunk] = (kept, partner(outgoing, "bfly", level % bit_count))
        if len(matrices) == level + 1 < LEVELS:
            following, token = split_matrices(token, transfers, level + 1)
            matrices.append(following)
    return result


def solution(mesh):
    return jax.shard_map(
        on_device,
        mesh=mesh,
        in_specs=(P("bfly", None, None), P("bfly", None, None, None, None)),
        out_specs=P("bfly", None, None),
        check_vma=False,
    )
```

```python
import functools
import jax
import jax.numpy as jnp
from jax import lax
from jax.experimental import pallas as pl
from jax.experimental.pallas import tpu as pltpu
from jax.sharding import PartitionSpec as P

LEVELS = 8
WIDTHS = (128, 128, 256, 256, 256)
ORDER = (
    (3, 0), (3, 1), (0, 0), (3, 2), (1, 0), (2, 0), (0, 1), (3, 3), (0, 2), (1, 1), (3, 4), (4, 0),
    (1, 2), (0, 3), (3, 5), (0, 4), (1, 3), (4, 1), (3, 6), (0, 5), (1, 4), (4, 2), (1, 5), (0, 6),
    (4, 3), (3, 7), (2, 1), (4, 4), (2, 2), (4, 5), (1, 6), (2, 3), (1, 7), (2, 4), (0, 7), (2, 5),
    (3, 8), (4, 6), (0, 8), (2, 6), (1, 8), (4, 7), (2, 7), (4, 8), (2, 8),
)
ANY = pl.BlockSpec(memory_space=pl.ANY)
VMEM = pl.BlockSpec(memory_space=pltpu.VMEM)
PARAMS = pltpu.CompilerParams(vmem_limit_bytes=12 << 20)
TOKEN = pltpu.VMEM((8, 128), jnp.float32)
COST = pl.CostEstimate(flops=1 << 33, bytes_accessed=1 << 10, transcendentals=0)


def partner(block, axis, stride):
    count = lax.axis_size(axis)
    route = []
    for low in range(count):
        high = low | 1 << stride
        if high != low and high < count:
            route += [(low, high), (high, low)]
    return lax.ppermute(block, axis, route)


def on_chip(values):
    return pltpu.with_memory_space_constraint(values, pltpu.VMEM)


def split(values):
    high = values.astype(jnp.bfloat16)
    return high, (values - high.astype(jnp.float32)).astype(jnp.bfloat16)


def in_hbm(values):
    return pltpu.with_memory_space_constraint(values, pltpu.HBM)


def split_kernel(token_ref, t_ref, out_ref, next_ref):
    rank = t_ref.shape[-1]
    rows = 16
    for which in range(2):
        @pl.loop(0, rank // rows)
        def _(i):
            here = pl.ds(pl.multiple_of(i * rows, rows), rows)
            there = pl.ds(pl.multiple_of(which * rank + i * rows, rows), rows)
            high, low = split(t_ref[0, 0, which, here])
            out_ref[there, :rank] = high
            out_ref[there, rank:2 * rank] = high
            out_ref[there, 2 * rank:] = low
    next_ref[...] = jnp.zeros_like(next_ref)


def split_matrices(token, transfers, level):
    rank = transfers.shape[-1]
    return pl.pallas_call(
        split_kernel,
        grid=(1,),
        out_shape=(pltpu.VMEM((2 * rank, 3 * rank), jnp.bfloat16), TOKEN),
        in_specs=[VMEM, pl.BlockSpec((1, 1, 2, rank, rank), lambda i: (0, level, 0, 0, 0))],
        out_specs=(VMEM, VMEM),
        cost_estimate=COST,
        compiler_params=PARAMS,
        name="split_matrices",
    )(on_chip(token), in_hbm(transfers))


def multiply(blocks, t_ref, part_refs, send_ref, keep_ref, stacked):
    rank = send_ref.shape[0]
    step = 48

    @pl.loop(0, rank // step)
    def _(i):
        here = pl.multiple_of(i * step, step)
        current = part_refs[0][pl.ds(here, step)]
        for part_ref in part_refs[1:]:
            current = current + part_ref[pl.ds(here, step)]
        high, low = split(current)
        stacked[pl.ds(here, step)] = high
        stacked[pl.ds(pl.multiple_of(here + rank, step), step)] = low
        stacked[pl.ds(pl.multiple_of(here + 2 * rank, step), step)] = high

    rows = rank // blocks

    @pl.loop(0, 2 * blocks)
    def _(i):
        source = pl.ds(pl.multiple_of(i * rows, rows), rows)
        product = jnp.dot(t_ref[source], stacked[...], preferred_element_type=jnp.float32)

        @pl.when(i < blocks)
        def _():
            keep_ref[source] = product

        @pl.when(i >= blocks)
        def _():
            send_ref[pl.ds(pl.multiple_of((i - blocks) * rows, rows), rows)] = product


def first_kernel(start, token_ref, t_ref, c_ref, send_ref, keep_ref, next_ref, stacked):
    block = c_ref.at[0, :, pl.ds(start, stacked.shape[1])]
    multiply(2, t_ref, (block,), send_ref, keep_ref, stacked)
    next_ref[...] = jnp.zeros_like(next_ref)


def level_kernel(token_ref, t_ref, kept_ref, arrived_ref, send_ref, keep_ref, next_ref, stacked):
    multiply(1, t_ref, (kept_ref, arrived_ref), send_ref, keep_ref, stacked)
    next_ref[...] = jnp.zeros_like(next_ref)


def stage(name, kernel, operands, specs, width):
    rank = operands[1].shape[0] // 2
    block = pltpu.VMEM((rank, width), jnp.float32)
    return pl.pallas_call(
        kernel,
        out_shape=(block, block, TOKEN),
        in_specs=specs,
        out_specs=(VMEM, VMEM, VMEM),
        scratch_shapes=[pltpu.VMEM((3 * rank, width), jnp.bfloat16)],
        cost_estimate=COST,
        compiler_params=PARAMS,
        name=name,
    )(*operands)


def first_level(token, matrices, coeffs, start, width):
    operands = tuple(map(on_chip, (token, matrices, coeffs)))
    return stage("first_level", functools.partial(first_kernel, start), operands, [VMEM] * 3, width)


def next_level(token, matrices, kept, arrived):
    operands = tuple(map(on_chip, (token, matrices, kept, arrived)))
    return stage("next_level", level_kernel, operands, [VMEM] * 4, kept.shape[1])


def write_kernel(start, token_ref, kept_ref, arrived_ref, *refs):
    out_ref, next_ref, block, sem = refs[-4:]
    step = 48

    @pl.loop(0, block.shape[0] // step)
    def _(i):
        here = pl.ds(pl.multiple_of(i * step, step), step)
        block[here] = kept_ref[here] + arrived_ref[here]

    copy = pltpu.make_async_copy(block, out_ref.at[0, :, pl.ds(start, block.shape[1])], sem)
    copy.start()
    copy.wait()
    next_ref[...] = jnp.zeros_like(next_ref)


def write_result(token, kept, arrived, start, shape, result):
    parts = tuple(map(on_chip, (token, kept, arrived))) + (() if result is None else (result,))
    return pl.pallas_call(
        functools.partial(write_kernel, start),
        out_shape=(jax.ShapeDtypeStruct(shape, jnp.float32), TOKEN),
        in_specs=[VMEM] * 3 + [ANY] * (len(parts) - 3),
        out_specs=(ANY, VMEM),
        scratch_shapes=[pltpu.VMEM(kept.shape, jnp.float32), pltpu.SemaphoreType.DMA],
        input_output_aliases={} if result is None else {3: 0},
        cost_estimate=COST,
        compiler_params=PARAMS,
        name="write_result",
    )(*parts)


def on_device(coeffs, transfers):
    bit_count = lax.axis_size("bfly").bit_length() - 1
    starts = [sum(WIDTHS[:i]) for i in range(len(WIDTHS))]
    parts = [()] * len(WIDTHS)
    token = jnp.zeros(TOKEN.shape, TOKEN.dtype)
    first, token = split_matrices(token, transfers, 0)
    matrices = [first]
    result = None
    for chunk, level in ORDER:
        if level == LEVELS:
            result, token = write_result(token, *parts[chunk], starts[chunk], coeffs.shape, result)
            continue
        if level == 0:
            stepped = first_level(token, matrices[0], coeffs, starts[chunk], WIDTHS[chunk])
        else:
            stepped = next_level(token, matrices[level], *parts[chunk])
        outgoing, kept, token = stepped
        parts[chunk] = (kept, partner(outgoing, "bfly", level % bit_count))
        if len(matrices) == level + 1 < LEVELS:
            following, token = split_matrices(token, transfers, level + 1)
            matrices.append(following)
    return result


def solution(mesh):
    return jax.shard_map(
        on_device,
        mesh=mesh,
        in_specs=(P("bfly", None, None), P("bfly", None, None, None, None)),
        out_specs=P("bfly", None, None),
        check_vma=False,
    )
```

```python
import functools
import jax
import jax.numpy as jnp
from jax import lax
from jax.experimental import pallas as pl
from jax.experimental.pallas import tpu as pltpu
from jax.sharding import PartitionSpec as P

LEVELS = 8
WIDTHS = (256, 128, 128, 256, 256)
ORDER = (
    (0, 0), (0, 1), (0, 2), (1, 0), (0, 3), (1, 1), (2, 1), (0, 4), (1, 2), (2, 2), (1, 3), (0, 5),
    (2, 3), (4, 1), (1, 4), (0, 6), (1, 5), (4, 2), (2, 4), (1, 6), (2, 5), (4, 3), (0, 7), (3, 1),
    (4, 4), (3, 2), (4, 5), (2, 6), (3, 3), (2, 7), (3, 4), (1, 7), (3, 5), (4, 6), (0, 8), (2, 8),
    (3, 6), (1, 8), (4, 7), (3, 7), (4, 8), (3, 8),
)
LAST = {0: 0, 1: 4}
ANY = pl.BlockSpec(memory_space=pl.ANY)
VMEM = pl.BlockSpec(memory_space=pltpu.VMEM)
PARAMS = pltpu.CompilerParams(vmem_limit_bytes=12 << 20)
TOKEN = pltpu.VMEM((8, 128), jnp.float32)
COST = pl.CostEstimate(flops=1 << 33, bytes_accessed=1 << 10, transcendentals=0)


def partner(block, axis, stride):
    count = lax.axis_size(axis)
    route = []
    for low in range(count):
        high = low | 1 << stride
        if high != low and high < count:
            route += [(low, high), (high, low)]
    return lax.ppermute(block, axis, route)


def on_chip(values):
    return pltpu.with_memory_space_constraint(values, pltpu.VMEM)


def split(values):
    high = values.astype(jnp.bfloat16)
    return high, (values - high.astype(jnp.float32)).astype(jnp.bfloat16)


def in_hbm(values):
    return pltpu.with_memory_space_constraint(values, pltpu.HBM)


def split_kernel(token_ref, t_ref, out_ref, next_ref):
    rank = t_ref.shape[-1]
    rows = 16
    for which in range(2):
        @pl.loop(0, rank // rows)
        def _(i):
            here = pl.ds(pl.multiple_of(i * rows, rows), rows)
            there = pl.ds(pl.multiple_of(which * rank + i * rows, rows), rows)
            high, low = split(t_ref[0, 0, which, here])
            out_ref[there, :rank] = high
            out_ref[there, rank:2 * rank] = high
            out_ref[there, 2 * rank:] = low
    next_ref[...] = jnp.zeros_like(next_ref)


def split_matrices(token, transfers, level):
    rank = transfers.shape[-1]
    return pl.pallas_call(
        split_kernel,
        grid=(1,),
        out_shape=(pltpu.VMEM((2 * rank, 3 * rank), jnp.bfloat16), TOKEN),
        in_specs=[VMEM, pl.BlockSpec((1, 1, 2, rank, rank), lambda i: (0, level, 0, 0, 0))],
        out_specs=(VMEM, VMEM),
        cost_estimate=COST,
        compiler_params=PARAMS,
        name="split_matrices",
    )(on_chip(token), in_hbm(transfers))


def multiply(blocks, t_ref, part_refs, send_ref, keep_ref, stacked):
    rank = send_ref.shape[0]
    step = 48

    @pl.loop(0, rank // step)
    def _(i):
        here = pl.multiple_of(i * step, step)
        current = part_refs[0][pl.ds(here, step)]
        for part_ref in part_refs[1:]:
            current = current + part_ref[pl.ds(here, step)]
        high, low = split(current)
        stacked[pl.ds(here, step)] = high
        stacked[pl.ds(pl.multiple_of(here + rank, step), step)] = low
        stacked[pl.ds(pl.multiple_of(here + 2 * rank, step), step)] = high

    rows = rank // blocks

    @pl.loop(0, 2 * blocks)
    def _(i):
        source = pl.ds(pl.multiple_of(i * rows, rows), rows)
        product = jnp.dot(t_ref[source], stacked[...], preferred_element_type=jnp.float32)

        @pl.when(i < blocks)
        def _():
            keep_ref[source] = product

        @pl.when(i >= blocks)
        def _():
            send_ref[pl.ds(pl.multiple_of((i - blocks) * rows, rows), rows)] = product


def first_kernel(start, token_ref, t_ref, c_ref, send_ref, keep_ref, next_ref, stacked):
    block = c_ref.at[0, :, pl.ds(start, stacked.shape[1])]
    multiply(1, t_ref, (block,), send_ref, keep_ref, stacked)
    next_ref[...] = jnp.zeros_like(next_ref)


def level_kernel(start, token_ref, t_ref, kept_ref, arrived_ref, send_ref, keep_ref, next_ref, stacked):
    columns = pl.ds(start, stacked.shape[1])
    parts = (kept_ref.at[:, columns], arrived_ref.at[:, columns])
    multiply(1, t_ref, parts, send_ref, keep_ref, stacked)
    next_ref[...] = jnp.zeros_like(next_ref)


def stage(name, kernel, operands, specs, width):
    rank = operands[1].shape[0] // 2
    block = pltpu.VMEM((rank, width), jnp.float32)
    return pl.pallas_call(
        kernel,
        out_shape=(block, block, TOKEN),
        in_specs=specs,
        out_specs=(VMEM, VMEM, VMEM),
        scratch_shapes=[pltpu.VMEM((3 * rank, width), jnp.bfloat16)],
        cost_estimate=COST,
        compiler_params=PARAMS,
        name=name,
    )(*operands)


def first_level(token, matrices, coeffs, start, width):
    operands = tuple(map(on_chip, (token, matrices, coeffs)))
    return stage("first_level", functools.partial(first_kernel, start), operands, [VMEM] * 3, width)


def next_level(token, matrices, kept, arrived, start, width):
    operands = tuple(map(on_chip, (token, matrices, kept, arrived)))
    return stage("next_level", functools.partial(level_kernel, start), operands, [VMEM] * 4, width)


def write_kernel(start, token_ref, kept_ref, arrived_ref, *refs):
    out_ref, next_ref, block, sem = refs[-4:]
    step = 48

    @pl.loop(0, block.shape[0] // step)
    def _(i):
        here = pl.ds(pl.multiple_of(i * step, step), step)
        block[here] = kept_ref[here] + arrived_ref[here]

    copy = pltpu.make_async_copy(block, out_ref.at[0, :, pl.ds(start, block.shape[1])], sem)
    copy.start()
    copy.wait()
    next_ref[...] = jnp.zeros_like(next_ref)


def write_result(token, kept, arrived, start, shape, result):
    parts = tuple(map(on_chip, (token, kept, arrived))) + (() if result is None else (result,))
    return pl.pallas_call(
        functools.partial(write_kernel, start),
        out_shape=(jax.ShapeDtypeStruct(shape, jnp.float32), TOKEN),
        in_specs=[VMEM] * 3 + [ANY] * (len(parts) - 3),
        out_specs=(ANY, VMEM),
        scratch_shapes=[pltpu.VMEM(kept.shape, jnp.float32), pltpu.SemaphoreType.DMA],
        input_output_aliases={} if result is None else {3: 0},
        cost_estimate=COST,
        compiler_params=PARAMS,
        name="write_result",
    )(*parts)


def on_device(coeffs, transfers):
    bit_count = lax.axis_size("bfly").bit_length() - 1
    starts = [sum(WIDTHS[:i]) for i in range(len(WIDTHS))]
    parts = [()] * len(WIDTHS)
    token = jnp.zeros(TOKEN.shape, TOKEN.dtype)
    first, token = split_matrices(token, transfers, 0)
    matrices = [first]
    result = None
    for chunk, level in ORDER:
        start, width = starts[chunk], WIDTHS[chunk]
        if level == LEVELS:
            result, token = write_result(token, *parts[chunk][:2], start, coeffs.shape, result)
            continue
        if level == 0:
            last = LAST[chunk]
            width = starts[last] + WIDTHS[last] - start
            stepped = first_level(token, matrices[0], coeffs, start, width)
        else:
            kept, arrived, base = parts[chunk]
            stepped = next_level(token, matrices[level], kept, arrived, start - base, width)
        outgoing, kept, token = stepped
        arrived = partner(outgoing, "bfly", level % bit_count)
        for member in range(chunk, LAST[chunk] + 1) if level == 0 else (chunk,):
            parts[member] = (kept, arrived, start)
        if len(matrices) == level + 1 < LEVELS:
            following, token = split_matrices(token, transfers, level + 1)
            matrices.append(following)
    return result


def solution(mesh):
    return jax.shard_map(
        on_device,
        mesh=mesh,
        in_specs=(P("bfly", None, None), P("bfly", None, None, None, None)),
        out_specs=P("bfly", None, None),
        check_vma=False,
    )
```

```python
import functools
import jax
import jax.numpy as jnp
from jax import lax
from jax.experimental import pallas as pl
from jax.experimental.pallas import tpu as pltpu
from jax.sharding import PartitionSpec as P

LEVELS = 8
WIDTHS = (256, 128, 128, 256, 256)
ORDER = (
    (0, 0), (0, 1), (0, 2), (1, 0), (0, 3), (1, 1), (2, 1), (0, 4), (1, 2), (2, 2), (1, 3), (0, 5),
    (2, 3), (4, 1), (1, 4), (0, 6), (1, 5), (4, 2), (2, 4), (1, 6), (2, 5), (4, 3), (0, 7), (3, 1),
    (4, 4), (3, 2), (4, 5), (2, 6), (3, 3), (2, 7), (3, 4), (1, 7), (3, 5), (4, 6), (0, 8), (2, 8),
    (3, 6), (1, 8), (4, 7), (3, 7), (4, 8), (3, 8),
)
LAST = {0: 0, 1: 4}
ANY = pl.BlockSpec(memory_space=pl.ANY)
VMEM = pl.BlockSpec(memory_space=pltpu.VMEM)
PARAMS = pltpu.CompilerParams(vmem_limit_bytes=12 << 20)
TOKEN = pltpu.VMEM((8, 128), jnp.float32)
COST = pl.CostEstimate(flops=1 << 33, bytes_accessed=1 << 10, transcendentals=0)


def partner(block, axis, stride):
    count = lax.axis_size(axis)
    route = []
    for low in range(count):
        high = low | 1 << stride
        if high != low and high < count:
            route += [(low, high), (high, low)]
    return lax.ppermute(block, axis, route)


def on_chip(values):
    return pltpu.with_memory_space_constraint(values, pltpu.VMEM)


def split(values):
    high = values.astype(jnp.bfloat16)
    return high, (values - high.astype(jnp.float32)).astype(jnp.bfloat16)


def in_hbm(values):
    return pltpu.with_memory_space_constraint(values, pltpu.HBM)


def split_kernel(token_ref, t_ref, out_ref, next_ref):
    rank = t_ref.shape[-1]
    rows = 16
    for which in range(2):
        @pl.loop(0, rank // rows)
        def _(i):
            here = pl.ds(pl.multiple_of(i * rows, rows), rows)
            there = pl.ds(pl.multiple_of(which * rank + i * rows, rows), rows)
            high, low = split(t_ref[0, 0, which, here])
            out_ref[there, :rank] = high
            out_ref[there, rank:2 * rank] = high
            out_ref[there, 2 * rank:] = low
    next_ref[...] = jnp.zeros_like(next_ref)


def split_matrices(token, transfers, level):
    rank = transfers.shape[-1]
    return pl.pallas_call(
        split_kernel,
        grid=(1,),
        out_shape=(pltpu.VMEM((2 * rank, 3 * rank), jnp.bfloat16), TOKEN),
        in_specs=[VMEM, pl.BlockSpec((1, 1, 2, rank, rank), lambda i: (0, level, 0, 0, 0))],
        out_specs=(VMEM, VMEM),
        cost_estimate=COST,
        compiler_params=PARAMS,
        name="split_matrices",
    )(on_chip(token), in_hbm(transfers))


def multiply(blocks, t_ref, part_refs, send_ref, keep_ref, stacked):
    rank = send_ref.shape[0]
    step = 128

    @pl.loop(0, rank // step)
    def _(i):
        here = pl.multiple_of(i * step, step)
        current = part_refs[0][pl.ds(here, step)]
        for part_ref in part_refs[1:]:
            current = current + part_ref[pl.ds(here, step)]
        high, low = split(current)
        stacked[pl.ds(here, step)] = high
        stacked[pl.ds(pl.multiple_of(here + rank, step), step)] = low
        stacked[pl.ds(pl.multiple_of(here + 2 * rank, step), step)] = high

    rows = rank // blocks

    @pl.loop(0, 2 * blocks)
    def _(i):
        source = pl.ds(pl.multiple_of(i * rows, rows), rows)
        product = jnp.dot(t_ref[source], stacked[...], preferred_element_type=jnp.float32)

        @pl.when(i < blocks)
        def _():
            keep_ref[source] = product

        @pl.when(i >= blocks)
        def _():
            send_ref[pl.ds(pl.multiple_of((i - blocks) * rows, rows), rows)] = product


def first_kernel(start, token_ref, t_ref, c_ref, send_ref, keep_ref, next_ref, stacked):
    block = c_ref.at[0, :, pl.ds(start, stacked.shape[1])]
    multiply(1, t_ref, (block,), send_ref, keep_ref, stacked)
    next_ref[...] = jnp.zeros_like(next_ref)


def level_kernel(start, token_ref, t_ref, kept_ref, arrived_ref, send_ref, keep_ref, next_ref, stacked):
    columns = pl.ds(start, stacked.shape[1])
    parts = (kept_ref.at[:, columns], arrived_ref.at[:, columns])
    multiply(1, t_ref, parts, send_ref, keep_ref, stacked)
    next_ref[...] = jnp.zeros_like(next_ref)


def stage(name, kernel, operands, specs, width):
    rank = operands[1].shape[0] // 2
    block = pltpu.VMEM((rank, width), jnp.float32)
    return pl.pallas_call(
        kernel,
        out_shape=(block, block, TOKEN),
        in_specs=specs,
        out_specs=(VMEM, VMEM, VMEM),
        scratch_shapes=[pltpu.VMEM((3 * rank, width), jnp.bfloat16)],
        cost_estimate=COST,
        compiler_params=PARAMS,
        name=name,
    )(*operands)


def first_level(token, matrices, coeffs, start, width):
    operands = tuple(map(on_chip, (token, matrices, coeffs)))
    return stage("first_level", functools.partial(first_kernel, start), operands, [VMEM] * 3, width)


def next_level(token, matrices, kept, arrived, start, width):
    operands = tuple(map(on_chip, (token, matrices, kept, arrived)))
    return stage("next_level", functools.partial(level_kernel, start), operands, [VMEM] * 4, width)


def write_kernel(start, token_ref, kept_ref, arrived_ref, *refs):
    out_ref, next_ref, block, sem = refs[-4:]
    step = 128

    @pl.loop(0, block.shape[0] // step)
    def _(i):
        here = pl.ds(pl.multiple_of(i * step, step), step)
        block[here] = kept_ref[here] + arrived_ref[here]

    copy = pltpu.make_async_copy(block, out_ref.at[0, :, pl.ds(start, block.shape[1])], sem)
    copy.start()
    copy.wait()
    next_ref[...] = jnp.zeros_like(next_ref)


def write_result(token, kept, arrived, start, shape, result):
    parts = tuple(map(on_chip, (token, kept, arrived))) + (() if result is None else (result,))
    return pl.pallas_call(
        functools.partial(write_kernel, start),
        out_shape=(jax.ShapeDtypeStruct(shape, jnp.float32), TOKEN),
        in_specs=[VMEM] * 3 + [ANY] * (len(parts) - 3),
        out_specs=(ANY, VMEM),
        scratch_shapes=[pltpu.VMEM(kept.shape, jnp.float32), pltpu.SemaphoreType.DMA],
        input_output_aliases={} if result is None else {3: 0},
        cost_estimate=COST,
        compiler_params=PARAMS,
        name="write_result",
    )(*parts)


def on_device(coeffs, transfers):
    bit_count = lax.axis_size("bfly").bit_length() - 1
    starts = [sum(WIDTHS[:i]) for i in range(len(WIDTHS))]
    parts = [()] * len(WIDTHS)
    token = jnp.zeros(TOKEN.shape, TOKEN.dtype)
    first, token = split_matrices(token, transfers, 0)
    matrices = [first]
    result = None
    for chunk, level in ORDER:
        start, width = starts[chunk], WIDTHS[chunk]
        if level == LEVELS:
            result, token = write_result(token, *parts[chunk][:2], start, coeffs.shape, result)
            continue
        if level == 0:
            last = LAST[chunk]
            width = starts[last] + WIDTHS[last] - start
            stepped = first_level(token, matrices[0], coeffs, start, width)
        else:
            kept, arrived, base = parts[chunk]
            stepped = next_level(token, matrices[level], kept, arrived, start - base, width)
        outgoing, kept, token = stepped
        arrived = partner(outgoing, "bfly", level % bit_count)
        for member in range(chunk, LAST[chunk] + 1) if level == 0 else (chunk,):
            parts[member] = (kept, arrived, start)
        if len(matrices) == level + 1 < LEVELS:
            following, token = split_matrices(token, transfers, level + 1)
            matrices.append(following)
    return result


def solution(mesh):
    return jax.shard_map(
        on_device,
        mesh=mesh,
        in_specs=(P("bfly", None, None), P("bfly", None, None, None, None)),
        out_specs=P("bfly", None, None),
        check_vma=False,
    )
```
